256 devices in a mesh: tab: 64 (over y, z, core), col: 4 (over x).
Axes of the slice: x: 4, y: 4, z: 8, core: 2. Of those that a mesh axis runs over, the one named last changes fastest.
Arguments:
- bag_items: bfloat16 [128, 4, 48, 8192], P('tab', None, 'col'), may hold values from -3 to 3
- lengths: int32 [128, 8192], P('tab'), may hold values from 1 to 4
- field_slot: int32 [64], replicated, may hold values from 0 to 127, as said below
- filter_one: bfloat16 [32, 4096], replicated, may hold values from -0.09375 to 0.09375
- filter_two: bfloat16 [32, 2048], replicated, may hold values from -0.125 to 0.125
- cotangent: bfloat16 [64, 8192], P(None, ('tab', 'col')), may hold values from -12 to 12
Outputs:
- pooled: float32 [64, 8192], P(None, ('tab', 'col'))
- filter_grad_one: float32 [32, 4096], P(None, ('tab', 'col'))
- filter_grad_two: float32 [32, 2048], P(None, ('tab', 'col'))
- pooled_grad: bfloat16 [128, 48, 8192], P('tab', 'col')
The draws below stay inside these ranges and needn't reach their ends.
Inputs may be any that keep to these rules, and one draw needn't show every extreme that they name: Distinct values; the table of field f is held by index field_slot[f] // 2 of tab; owners hold 0 to 2 fields and one owner holds 2.
All inputs are finite; a program needn't handle non-finite values.
Results may differ from the reference program's by a relative error of at most 0.017.
Values may be sent and summed in bfloat16 or wider, within the bound.
A program may use at most 64 MiB of HBM per device.

```python
import jax
import jax.numpy as jnp
from jax import lax

F = 64
D = 48
MAPS = 32
L_MAX = 4
SAMP_DEV = 128
SLOTS = 2
SAMPLES = 8192
N_TAB = 64


def draw_field_slot(key, part):
    slot_total = N_TAB * SLOTS
    owner_key, order_key, field_key = jax.random.split(jax.random.fold_in(key, 11), 3)
    full_owner = jax.random.randint(owner_key, (), 0, N_TAB)
    ranking = jax.random.permutation(order_key, slot_total).astype(jnp.int32)
    slot_index = jnp.arange(slot_total, dtype=jnp.int32)
    scores = jnp.where(slot_index // SLOTS == full_owner, slot_index - slot_total, ranking)
    chosen = jnp.argsort(scores, stable=True)[:F]
    shuffled = jax.random.permutation(field_key, F)
    return chosen[shuffled].astype(jnp.int32)


def plant(result, rng, smallest, largest):
    place = [jax.random.randint(jax.random.fold_in(rng, axis), (), 0, length) for axis, length in enumerate(result.shape)]
    widest = result.shape.index(max(result.shape))
    neighbour = place[:widest] + [(place[widest] + 1) % result.shape[widest]] + place[widest + 1:]
    return result.at[tuple(place)].set(smallest).at[tuple(neighbour)].set(largest)


def levels(key, extent, shards, low, top_value):
    def one(dim, shards_of):
        draws = jax.random.uniform(jax.random.fold_in(jax.random.fold_in(key, 6), dim), (shards_of,), jnp.float32, low / len(shards), top_value / len(shards))
        return jnp.repeat(jnp.exp(draws), extent[dim] // shards_of).reshape((-1,) + (1,) * (len(extent) - dim - 1))

    factor_of = one(*shards[0])
    for cut in shards[1:]:
        factor_of = factor_of * one(*cut)
    return factor_of


def bell_draw(own_key, shape, spread, bound, shards=(), kind=jnp.bfloat16):
    values = jax.random.normal(own_key, shape, jnp.float32) * spread
    if len(shards) > 0:
        values = levels(own_key, shape, shards, -0.22, 0.18) * values
    return jnp.clip(values, min=-bound, max=bound).astype(kind)


def setup_inputs(seed: int = 0) -> dict:
    arg_keys = jax.random.split(jax.random.key(seed), 7)
    return {
        "bag_items": bell_draw(arg_keys[0], (N_TAB * SLOTS, L_MAX, D, SAMPLES), 0.5, 3.0, ((0, 64), (2, 4))),
        "lengths": plant(jax.random.randint(arg_keys[1], (N_TAB * SLOTS, SAMPLES), 1, L_MAX + 1), jax.random.fold_in(arg_keys[1], 1), 1, L_MAX).astype(jnp.int32),
        "field_slot": draw_field_slot(jax.random.fold_in(arg_keys[6], 71), 0),
        "filter_one": bell_draw(arg_keys[3], (MAPS, F * F), (F * F) ** -0.5, 0.09375),
        "filter_two": bell_draw(arg_keys[4], (MAPS, MAPS * F), (MAPS * F) ** -0.5, 0.125),
        "cotangent": bell_draw(arg_keys[5], (2 * MAPS, SAMPLES), 2.0, 12.0, ((1, 256),)),
    }


def cross_block(first_cols, upstream, filter_one, filter_two):
    fields, columns = first_cols.shape
    map_count = filter_one.shape[0]
    first_pairs = (first_cols[:, None, :] * first_cols[None, :, :]).reshape(fields * fields, columns)
    first_maps = jnp.dot(filter_one, first_pairs, preferred_element_type=jnp.float32)
    hidden_cols = lax.optimization_barrier(first_maps.astype(jnp.bfloat16))
    second_pairs = (hidden_cols[:, None, :] * first_cols[None, :, :]).reshape(map_count * fields, columns)
    second_maps = jnp.dot(filter_two, second_pairs, preferred_element_type=jnp.float32)
    upper_grad = upstream[map_count:]
    grad_two = lax.dot_general(upper_grad, second_pairs, (((1,), (1,)), ((), ())), preferred_element_type=jnp.float32)
    pair_grad_two = lax.dot_general(filter_two, upper_grad, (((0,), (0,)), ((), ())), preferred_element_type=jnp.float32)
    pair_grad_two = lax.optimization_barrier(pair_grad_two.astype(jnp.bfloat16))
    pair_grad_two = pair_grad_two.reshape(map_count, fields, columns).astype(jnp.float32)
    first_float = first_cols.astype(jnp.float32)
    hidden_grad = jnp.sum(pair_grad_two * first_float[None], axis=1)
    field_grad = jnp.sum(pair_grad_two * hidden_cols.astype(jnp.float32)[:, None], axis=0)
    lower_grad = (upstream[:map_count].astype(jnp.float32) + hidden_grad).astype(jnp.bfloat16)
    grad_one = lax.dot_general(lower_grad, first_pairs, (((1,), (1,)), ((), ())), preferred_element_type=jnp.float32)
    pair_grad_one = lax.dot_general(filter_one, lower_grad, (((0,), (0,)), ((), ())), preferred_element_type=jnp.float32)
    pair_grad_one = lax.optimization_barrier(pair_grad_one.astype(jnp.bfloat16))
    pair_grad_one = pair_grad_one.reshape(fields, fields, columns).astype(jnp.float32)
    field_grad = field_grad + jnp.sum(pair_grad_one * first_float[None], axis=1) + jnp.sum(pair_grad_one * first_float[:, None], axis=0)
    return first_maps, second_maps, field_grad.astype(jnp.bfloat16), grad_one, grad_two


def reference(bag_items, lengths, field_slot, filter_one, filter_two, cotangent):
    item_index = jnp.arange(L_MAX)[None, :, None, None]
    kept_items = jnp.where(item_index < lengths[:, None, None, :], bag_items, jnp.zeros_like(bag_items))
    pooled_table = jnp.sum(kept_items.astype(jnp.float32), axis=1).astype(jnp.bfloat16)
    field_embed = pooled_table[field_slot]
    block_count = SAMPLES // SAMP_DEV
    embed_blocks = field_embed.reshape(F, D, block_count, SAMP_DEV).transpose(2, 0, 1, 3).reshape(block_count, F, D * SAMP_DEV)
    grad_blocks = cotangent.reshape(2 * MAPS, block_count, SAMP_DEV).transpose(1, 0, 2)

    def advance(totals, inputs):
        embed_cols, grad_cols = inputs
        upstream = jnp.broadcast_to(grad_cols[:, None, :], (2 * MAPS, D, SAMP_DEV)).astype(jnp.float32) * D ** -0.5
        upstream = upstream.astype(jnp.bfloat16).reshape(2 * MAPS, D * SAMP_DEV)
        first_maps, second_maps, field_grad, grad_one, grad_two = cross_block(embed_cols, upstream, filter_one, filter_two)
        both_maps = jnp.concatenate([first_maps, second_maps], axis=0).reshape(2 * MAPS, D, SAMP_DEV)
        pooled_cols = jnp.sum(both_maps, axis=1) * D ** -0.5
        return (totals[0] + grad_one, totals[1] + grad_two), (pooled_cols, field_grad)

    zero_sums = (jnp.zeros((MAPS, F * F), jnp.float32), jnp.zeros((MAPS, MAPS * F), jnp.float32))
    (grad_one, grad_two), (pooled_blocks, field_blocks) = lax.scan(advance, zero_sums, (embed_blocks, grad_blocks))
    pooled = pooled_blocks.transpose(1, 0, 2).reshape(2 * MAPS, SAMPLES)
    field_grad = field_blocks.reshape(block_count, F, D, SAMP_DEV).transpose(1, 2, 0, 3).reshape(F, D, SAMPLES)
    pooled_grad = jnp.zeros((N_TAB * SLOTS, D, SAMPLES), jnp.bfloat16).at[field_slot].set(field_grad)
    grad_scale = SAMPLES ** -0.5
    return pooled, grad_one * grad_scale, grad_two * grad_scale, pooled_grad
```

```python
import functools

import jax
import jax.numpy as jnp
from jax import lax
from jax.experimental import pallas as pl
from jax.experimental.pallas import tpu as pltpu
from jax.sharding import PartitionSpec as P

MESH = pl.DeviceIdType.MESH
BF = jnp.bfloat16
F32 = jnp.float32
VMEM = pltpu.VMEM
DMA = pltpu.SemaphoreType.DMA

TAB, COL, CORES, NZ, NY = 64, 4, 2, 8, 4
F, D, MAPS, ITEMS, SLOTS = 64, 48, 32, 4, 2
DL = D // COL
SAMP = 128
ROWS = SLOTS * DL
NB, BW = DL // 2, 2 * SAMP
HALF = F // 2
SCALE = D ** -0.5


def dot(a, b):
    return jnp.dot(a, b, preferred_element_type=F32)


def dot_nt(a, b):
    return lax.dot_general(a, b, (((1,), (1,)), ((), ())), preferred_element_type=F32)


def iota(shape, axis):
    return lax.broadcasted_iota(jnp.int32, shape, axis)


def send(src, dst, ssem, rsem, where):
    copy = pltpu.make_async_remote_copy(
        src_ref=src, dst_ref=dst, send_sem=ssem, recv_sem=rsem, device_id=where, device_id_type=MESH
    )
    copy.start()


def wait_send(src, dst, ssem, rsem, where):
    pltpu.make_async_remote_copy(
        src_ref=src, dst_ref=dst, send_sem=ssem, recv_sem=rsem, device_id=where, device_id_type=MESH
    ).wait_send()


def wait_recv(src, dst, ssem, rsem, where):
    pltpu.make_async_remote_copy(
        src_ref=src, dst_ref=dst, send_sem=ssem, recv_sem=rsem, device_id=where, device_id_type=MESH
    ).wait_recv()


def greet(me, col):
    barrier = pltpu.get_barrier_semaphore()

    def along_tab(k, _):
        pl.semaphore_signal(
            barrier, inc=1, device_id={"tab": lax.rem(me + k, TAB)}, device_id_type=MESH
        )
        return 0

    lax.fori_loop(1, TAB, along_tab, 0)
    for k in range(1, COL):
        pl.semaphore_signal(
            barrier, inc=1, device_id={"col": lax.rem(col + k, COL)}, device_id_type=MESH
        )
    return barrier


def gather_kernel(bag, lengths, cot, recv, up, snd, cots, ssem, rsem, csend, crecv, lsem):
    me = lax.axis_index("tab")
    col = lax.axis_index("col")
    barrier = greet(me, col)

    def pool(dst, _):
        at = pl.ds(pl.multiple_of(dst * SAMP, SAMP), SAMP)
        halves = []
        for slot in range(SLOTS):
            count = lengths[pl.ds(slot, 1), at]
            total = jnp.zeros((DL, SAMP), F32)
            for item in range(ITEMS):
                value = bag[slot, item, :, at].astype(F32)
                total = total + jnp.where(count > item, value, 0.0)
            halves.append(total)
        snd[dst] = jnp.concatenate(halves, axis=0).astype(BF)
        return 0

    lax.fori_loop(0, TAB, pool, 0)
    cots[col] = cot[...]
    pl.semaphore_wait(barrier, TAB - 1 + COL - 1)
    for k in range(1, COL):
        to = lax.rem(col + k, COL)
        send(cots.at[col], cots.at[col], csend.at[k], crecv.at[col], {"col": to})

    def issue(k, _):
        to = lax.rem(me + k, TAB)
        send(snd.at[to], recv.at[me], ssem.at[to], rsem.at[me], {"tab": to})
        return 0

    lax.fori_loop(1, TAB, issue, 0)
    own = pltpu.make_async_copy(snd.at[me], recv.at[me], lsem)
    own.start()
    for k in range(1, COL):
        to = lax.rem(col + k, COL)
        wait_recv(cots.at[to], cots.at[to], csend.at[k], crecv.at[to], {"col": to})
    wide = jnp.concatenate([cots[c] for c in range(COL)], axis=1)
    up[...] = (wide.astype(F32) * SCALE).astype(BF)
    own.wait()

    def drain(k, _):
        to = lax.rem(me + k, TAB)
        wait_send(snd.at[to], recv.at[me], ssem.at[to], rsem.at[me], {"tab": to})
        wait_recv(snd.at[to], recv.at[to], ssem.at[to], rsem.at[to], {"tab": to})
        return 0

    lax.fori_loop(1, TAB, drain, 0)
    for k in range(1, COL):
        to = lax.rem(col + k, COL)
        wait_send(cots.at[col], cots.at[col], csend.at[k], crecv.at[col], {"col": to})


def cross_kernel(
    fslot, recv, up, f1, f2, table, grads, pooled, za, lz, hot, es, egs, ef, tw, hf, hg, eg, zy, acc, pacc
):
    lane = iota((MAPS, 2 * F), 1)
    even = (lane < F).astype(BF)
    odd = (lane >= F).astype(BF)
    for t in range(HALF):
        first = f1[:, 2 * F * t : 2 * F * (t + 1)]
        second = f2[:, 2 * F * (t // 2) : 2 * F * (t // 2 + 1)]
        za[t, 0:32] = first * even
        za[t, 32:64] = first * odd
        za[t, 64:96] = second * (odd if t % 2 else even)
        za[t, 96:128] = jnp.zeros((MAPS, 2 * F), BF)
    zy[...] = jnp.zeros(zy.shape, BF)
    acc[...] = jnp.zeros(acc.shape, F32)
    pacc[...] = jnp.zeros(pacc.shape, F32)
    fold = (iota((F, 2 * F), 0) == lax.rem(iota((F, 2 * F), 1), F)).astype(F32).astype(BF)
    for q in range(8):
        part = za[4 * q : 4 * q + 4].reshape(512, 2 * F)
        lz[:, 512 * q : 512 * (q + 1)] = dot_nt(fold, part).astype(BF)

    fs = fslot[...]
    diag = iota((F, F), 0) == iota((F, F), 1)
    fcol = jnp.sum(jnp.where(diag, jnp.broadcast_to(fs, (F, F)), 0).astype(F32), axis=1, keepdims=True)
    fcol = fcol.astype(jnp.int32) * DL
    slot_row = iota((F, TAB * ROWS), 1)
    for d in range(DL):
        hot[pl.ds(F * d, F), :] = (slot_row == fcol + d).astype(F32).astype(BF)
    for q in range(3):
        got = dot(hot[pl.ds(256 * q, 256), :], recv[...]).astype(BF)
        for k in range(2):
            es[2 * q + k] = jnp.concatenate(
                [got[128 * k : 128 * k + 64], got[128 * k + 64 : 128 * k + 128]], axis=1
            )

    u = up[...].astype(F32)
    u = jnp.concatenate([u, u], axis=1)
    u1, u2 = u[:MAPS], u[MAPS:]
    r = iota((F, F), 0)
    source = 32 * (lax.rem(r, 16) // 8) + 8 * (r // 16) + lax.rem(r, 8)
    perm = (source == iota((F, F), 1)).astype(F32).astype(BF)

    def block(b, _):
        e = es[b]
        ef[...] = e.astype(F32)
        ee = jnp.concatenate([e, e], axis=0)
        for q in range(8):
            part = za[4 * q : 4 * q + 4].reshape(512, 2 * F)
            tw[4 * q : 4 * q + 4] = dot(part, ee).reshape(4, 128, BW)

        def first(t, m1):
            m1 = m1 + tw[t, 0:32] * ef[pl.ds(2 * t, 1)] + tw[t, 32:64] * ef[pl.ds(2 * t + 1, 1)]
            hg[pl.ds(t, 1)] = jnp.sum(tw[t, 64:96] * u2, axis=0, keepdims=True)
            return m1

        m1 = lax.fori_loop(0, HALF, first, jnp.zeros((MAPS, BW), F32), unroll=4)
        hf[...] = m1.astype(BF).astype(F32)
        lg = (u1 + hg[...]).astype(BF).astype(F32)

        def second(t, m2):
            hrow = hf[pl.ds(t, 1)]
            m2 = m2 + tw[t, 64:96] * hrow
            eg[pl.ds(2 * t, 1)] = jnp.sum(tw[t, 0:32] * lg, axis=0, keepdims=True)
            eg[pl.ds(2 * t + 1, 1)] = jnp.sum(tw[t, 32:64] * lg, axis=0, keepdims=True)
            zy[t, 0:32] = (lg * ef[pl.ds(2 * t, 1)]).astype(BF)
            zy[t, 32:64] = (lg * ef[pl.ds(2 * t + 1, 1)]).astype(BF)
            zy[t, 64:96] = (u2 * hrow).astype(BF)
            return m2

        m2 = lax.fori_loop(0, HALF, second, jnp.zeros((MAPS, BW), F32), unroll=4)
        pacc[0:MAPS] += m1
        pacc[MAPS:] += m2
        eperm = dot(perm, e).astype(BF)
        e2 = jnp.concatenate([e, eperm], axis=0)
        low = lax.rem(iota((F, 512), 1), 128) < F
        back = eg[...]
        for q in range(8):
            part = zy[4 * q : 4 * q + 4].reshape(512, BW)
            back = back + dot(lz[:, 512 * q : 512 * (q + 1)], part)
            both = dot_nt(e2, part)
            acc[:, 512 * q : 512 * (q + 1)] += jnp.where(low, both[:F], both[F:])
        back = back.astype(BF)
        egs[pl.ds(pl.multiple_of(128 * b, 128), 64)] = back[:, :SAMP]
        egs[pl.ds(pl.multiple_of(128 * b + 64, 64), 64)] = back[:, SAMP:]
        return 0

    lax.fori_loop(0, NB, block, 0)
    pooled[...] = (pacc[:, :SAMP] + pacc[:, SAMP:]) * SCALE
    grads[...] = acc[...].astype(BF)
    two = jnp.concatenate([fs, fs], axis=1) * DL + (iota((1, 2 * F), 1) >= F).astype(jnp.int32)
    for q in range(3):
        row = iota((512, 2 * F), 0) + 512 * q
        hots = [(row == two + 2 * k).astype(F32).astype(BF) for k in range(NB)]
        table[pl.ds(512 * q, 512), :] = dot(jnp.concatenate(hots, axis=1), egs[...]).astype(BF)


def scatter_kernel(
    table, grads, pooled, out, g1, g2, pout,
    back, xr, yr, zr, pr, ysend, fin, ssem, rsem, xs, xv, ps, pv, ys, yv, zs, zv, lsem,
):
    me = lax.axis_index("tab")
    col = lax.axis_index("col")
    core = lax.rem(me, CORES)
    z = lax.rem(me // CORES, NZ)
    y = me // (CORES * NZ)
    barrier = greet(me, col)
    pl.semaphore_wait(barrier, TAB - 1 + COL - 1)

    for k in range(1, COL):
        to = lax.rem(col + k, COL)
        rows = pl.ds(pl.multiple_of(16 * to, 16), 16)
        send(grads.at[rows], xr.at[col], xs.at[k], xv.at[col], {"col": to})
        send(pooled, pr.at[col], ps.at[k], pv.at[col], {"col": to})

    def issue(k, _):
        to = lax.rem(me + k, TAB)
        send(table.at[to], back.at[me], ssem.at[to], rsem.at[me], {"tab": to})
        return 0

    lax.fori_loop(1, TAB, issue, 0)
    own = pltpu.make_async_copy(table.at[me], back.at[me], lsem)
    own.start()

    xr[col] = grads[pl.ds(pl.multiple_of(16 * col, 16), 16)]
    pr[col] = pooled[...]
    for k in range(1, COL):
        to = lax.rem(col + k, COL)
        wait_recv(xr.at[to], xr.at[to], xs.at[k], xv.at[to], {"col": to})
    for c in range(NY):
        at = pl.ds(1024 * c, 1024)
        ysend[c] = (
            (xr[0, :, at].astype(F32) + xr[1, :, at].astype(F32))
            + (xr[2, :, at].astype(F32) + xr[3, :, at].astype(F32))
        )
    for k in range(1, NY):
        to = lax.rem(y + k, NY)
        send(ysend.at[to], yr.at[y], ys.at[k], yv.at[y], {"tab": (to * NZ + z) * CORES + core})
    yr[y] = ysend[y]
    for k in range(1, COL):
        to = lax.rem(col + k, COL)
        wait_recv(pr.at[to], pr.at[to], ps.at[k], pv.at[to], {"col": to})
    total = (pr[0] + pr[1]) + (pr[2] + pr[3])
    mine = jnp.zeros((2 * MAPS, SAMP // COL), F32)
    for c in range(COL):
        mine = mine + jnp.where(col == c, total[:, 32 * c : 32 * c + 32], 0.0)
    pout[...] = mine
    for k in range(1, NY):
        to = lax.rem(y + k, NY)
        wait_recv(yr.at[to], yr.at[to], ys.at[k], yv.at[to], {"tab": (to * NZ + z) * CORES + core})
    for c in range(NZ):
        at = pl.ds(128 * c, 128)
        fin[c] = (yr[0, :, at] + yr[1, :, at]) + (yr[2, :, at] + yr[3, :, at])
    group = NZ * CORES
    place = z * CORES + core
    base = y * group
    for k in range(1, group):
        to = lax.rem(place + k, group)
        send(fin.at[to // CORES], zr.at[place], zs.at[k], zv.at[place], {"tab": base + to})
    zr[place] = fin[z]
    for k in range(1, group):
        to = lax.rem(place + k, group)
        wait_recv(zr.at[to], zr.at[to], zs.at[k], zv.at[to], {"tab": base + to})
    parts = [zr[k] for k in range(group)]
    while len(parts) > 1:
        parts = [parts[i] + parts[i + 1] for i in range(0, len(parts), 2)]
    done = parts[0] * (8192 ** -0.5)
    swapped = jnp.transpose(jnp.concatenate([done, jnp.zeros((112, 128), F32)], axis=0))
    g1[...] = jnp.where(core == 0, swapped[0:32, 0:16], swapped[32:64, 0:16])
    g2[...] = jnp.where(core == 0, swapped[64:96, 0:8], swapped[64:96, 8:16])

    own.wait()

    def drain(k, _):
        to = lax.rem(me + k, TAB)
        wait_send(table.at[to], back.at[me], ssem.at[to], rsem.at[me], {"tab": to})
        wait_recv(table.at[to], back.at[to], ssem.at[to], rsem.at[to], {"tab": to})
        return 0

    lax.fori_loop(1, TAB, drain, 0)

    def place_out(src, _):
        at = pl.ds(pl.multiple_of(src * SAMP, SAMP), SAMP)
        value = back[src].astype(F32)
        out[0, :, at] = value[:DL].astype(BF)
        out[1, :, at] = value[DL:].astype(BF)
        return 0

    lax.fori_loop(0, TAB, place_out, 0)
    for k in range(1, COL):
        to = lax.rem(col + k, COL)
        rows = pl.ds(pl.multiple_of(16 * to, 16), 16)
        wait_send(grads.at[rows], xr.at[col], xs.at[k], xv.at[col], {"col": to})
        wait_send(pooled, pr.at[col], ps.at[k], pv.at[col], {"col": to})
    for k in range(1, NY):
        to = lax.rem(y + k, NY)
        wait_send(ysend.at[to], yr.at[y], ys.at[k], yv.at[y], {"tab": (to * NZ + z) * CORES + core})
    for k in range(1, group):
        to = lax.rem(place + k, group)
        wait_send(fin.at[to // CORES], zr.at[place], zs.at[k], zv.at[place], {"tab": base + to})


def vmem():
    return pl.BlockSpec(memory_space=VMEM)


def per_device(bag_items, lengths, field_slot, filter_one, filter_two, cotangent):
    shape = jax.ShapeDtypeStruct
    recv, up = pl.pallas_call(
        gather_kernel,
        out_shape=(shape((TAB, ROWS, SAMP), BF), shape((2 * MAPS, SAMP), BF)),
        in_specs=[vmem()] * 3,
        out_specs=[vmem()] * 2,
        scratch_shapes=[
            VMEM((TAB, ROWS, SAMP), BF),
            VMEM((COL, 2 * MAPS, SAMP // COL), BF),
            DMA((TAB,)), DMA((TAB,)), DMA((COL,)), DMA((COL,)), DMA,
        ],
        compiler_params=pltpu.CompilerParams(collective_id=0, has_side_effects=True),
        name="gather",
    )(bag_items, lengths, cotangent)
    table, grads, pooled = pl.pallas_call(
        cross_kernel,
        out_shape=(shape((TAB * ROWS, SAMP), BF), shape((F, 4096), BF), shape((2 * MAPS, SAMP), F32)),
        in_specs=[vmem()] * 5,
        out_specs=[vmem()] * 3,
        scratch_shapes=[
            VMEM((HALF, 128, 2 * F), BF),
            VMEM((F, 4096), BF),
            VMEM((DL * F, TAB * ROWS), BF),
            VMEM((NB, F, BW), BF),
            VMEM((DL * F, SAMP), BF),
            VMEM((F, BW), F32),
            VMEM((HALF, 128, BW), F32),
            VMEM((MAPS, BW), F32),
            VMEM((MAPS, BW), F32),
            VMEM((F, BW), F32),
            VMEM((HALF, 128, BW), BF),
            VMEM((F, 4096), F32),
            VMEM((2 * MAPS, BW), F32),
        ],
        name="cross",
    )(field_slot.reshape(1, F), recv.reshape(TAB * ROWS, SAMP), up, filter_one, filter_two)
    out, g1, g2, pout = pl.pallas_call(
        scatter_kernel,
        out_shape=(
            shape((SLOTS, DL, TAB * SAMP), BF),
            shape((MAPS, 16), F32),
            shape((MAPS, 8), F32),
            shape((2 * MAPS, SAMP // COL), F32),
        ),
        in_specs=[vmem()] * 3,
        out_specs=[vmem()] * 4,
        scratch_shapes=[
            VMEM((TAB, ROWS, SAMP), BF),
            VMEM((COL, 16, 4096), BF),
            VMEM((NY, 16, 1024), F32),
            VMEM((NZ * CORES, 16, 128), F32),
            VMEM((COL, 2 * MAPS, SAMP), F32),
            VMEM((NY, 16, 1024), F32),
            VMEM((NZ, 16, 128), F32),
            DMA((TAB,)), DMA((TAB,)),
            DMA((COL,)), DMA((COL,)), DMA((COL,)), DMA((COL,)),
            DMA((NY,)), DMA((NY,)), DMA((NZ * CORES,)), DMA((NZ * CORES,)), DMA,
        ],
        compiler_params=pltpu.CompilerParams(collective_id=1, has_side_effects=True),
        name="scatter",
    )(table.reshape(TAB, ROWS, SAMP), grads, pooled)
    return pout, g1, g2, out


def solution(mesh):
    in_specs = (P("tab", None, "col", None), P("tab", None), P(), P(), P(), P(None, ("tab", "col")))
    out_specs = (
        P(None, ("tab", "col")),
        P(None, ("tab", "col")),
        P(None, ("tab", "col")),
        P("tab", "col", None),
    )
    return jax.shard_map(
        per_device, mesh=mesh, in_specs=in_specs, out_specs=out_specs, check_vma=False
    )
```
